128 devices in a mesh: seq: 4 (over y_hi, core), fsdp: 32 (over z, x, y_lo).
Axes of the slice: x: 4, y: 4 (y_hi: 2, y_lo: 2; y = y_hi * 2 + y_lo), z: 4, core: 2. Of those that a mesh axis runs over, the one named last changes fastest.
Arguments:
- hidden_in: bfloat16 [2048, 16384], P('seq', 'fsdp'), may hold values from -6 to 6
- gain_in: float32 [16384], P('fsdp'), may hold values from 0.25 to 1.75
- w_query: bfloat16 [16384, 4096], P('fsdp'), may hold values from -0.046875 to 0.046875
- query_scale: float32 [4096], replicated, may hold values from 0.5 to 2
- w_key: bfloat16 [16384, 256], P('fsdp'), may hold values from -0.046875 to 0.046875
- key_scale: float32 [256], replicated, may hold values from 0.5 to 2
- w_value: bfloat16 [16384, 256], P('fsdp'), may hold values from -0.046875 to 0.046875
- value_scale: float32 [256], replicated, may hold values from 0.5 to 2
- w_out: bfloat16 [4096, 16384], P(None, 'fsdp'), may hold values from -0.125 to 0.125
- out_scale: float32 [16384], P('fsdp'), may hold values from 0.5 to 2
- gain_mid: float32 [16384], P('fsdp'), may hold values from 0.25 to 1.75
- head_order: int32 [32], replicated, may hold values from 0 to 31, each once
Outputs:
- hessian: float32 [16384, 16384], P('fsdp', 'seq')
- residual_out: bfloat16 [2048, 16384], P('seq', 'fsdp')
The draws below stay inside these ranges and needn't reach their ends.
All inputs are finite; a program needn't handle non-finite values.
Results may differ from the reference program's by a relative error of at most 0.009.
Values may be sent and summed in bfloat16 or wider, within the bound.
No kernel may reach another device: no remote copies, remote signals or barrier semaphores. Data moves between devices by JAX's collectives and lax.ppermute only.
A program may use at most 128 MiB of HBM per device.

```python
import math
import jax
import jax.numpy as jnp
from jax import lax

D = 16384
HEAD = 128
GROUP = 16
KVW = 2
L = 256
HQ = 32
KEEP = 16
TOKENS = 2048


def level_of(own_key, shape, cuts, low, largest):
    level = 1.0
    for position, parts in cuts:
        steps = jax.random.uniform(jax.random.fold_in(jax.random.fold_in(own_key, 6), position), (parts,), jnp.float32, low / len(cuts), largest / len(cuts))
        level = level * jnp.repeat(jnp.exp(steps), shape[position] // parts).reshape((-1,) + (1,) * (len(shape) - 1 - position))
    return level


def scatter_about(own_key, extent, width, limit, pieces=(), held_as=jnp.bfloat16):
    entries = width * jax.random.normal(own_key, extent, jnp.float32)
    if pieces:
        entries = entries * level_of(own_key, extent, pieces, -0.22, 0.18)
    return jnp.clip(entries, -limit, limit).astype(held_as)


def setup_inputs(seed: int = 0) -> dict:
    streams_of = jax.random.split(jax.random.key(seed), 13)
    return {
        "hidden_in": scatter_about(streams_of[0], (TOKENS, D), 1.0, 6.0, ((0, 4), (1, 32))),
        "gain_in": jnp.clip(1.0 + 0.15 * jax.random.normal(streams_of[1], (D,), jnp.float32), 0.25, 1.75),
        "w_query": scatter_about(streams_of[2], (D, HQ * HEAD), D ** -0.5, 0.046875, ((0, 32),)),
        "query_scale": jnp.clip(jnp.exp(jax.random.uniform(streams_of[3], (HQ * HEAD,), jnp.float32, math.log(0.5), math.log(2.0))), 0.5, 2.0),
        "w_key": scatter_about(streams_of[4], (D, KVW * HEAD), D ** -0.5, 0.046875, ((0, 32),)),
        "key_scale": jnp.clip(jnp.exp(jax.random.uniform(streams_of[5], (KVW * HEAD,), jnp.float32, math.log(0.5), math.log(2.0))), 0.5, 2.0),
        "w_value": scatter_about(streams_of[6], (D, KVW * HEAD), D ** -0.5, 0.046875, ((0, 32),)),
        "value_scale": jnp.clip(jnp.exp(jax.random.uniform(streams_of[7], (KVW * HEAD,), jnp.float32, math.log(0.5), math.log(2.0))), 0.5, 2.0),
        "w_out": scatter_about(streams_of[8], (HQ * HEAD, D), (KEEP * HEAD) ** -0.5, 0.125, ((1, 32),)),
        "out_scale": jnp.clip(jnp.exp(math.log(2.0) - 1.3862944 * jax.random.uniform(streams_of[9], (D,), jnp.float32) ** level_of(streams_of[9], (D,), ((0, 32),), -0.2, 0.2)), 0.5, 2.0),
        "gain_mid": jnp.clip(1.0 + 0.15 * jax.random.normal(streams_of[10], (D,), jnp.float32), 0.25, 1.75),
        "head_order": jax.random.permutation(streams_of[11], HQ).astype(jnp.int32),
    }


epsilon = 1e-05

def rotate(values_in, positions):
    half_size = values_in.shape[-1] // 2
    steps_idx = jnp.arange(half_size, dtype=jnp.float32)
    frequency = jnp.exp(-jnp.log(jnp.float32(500000.0)) * steps_idx * 2.0 / values_in.shape[-1])
    angles = positions.astype(jnp.float32)[:, None] * frequency[None, :]
    cosine = jnp.cos(angles)[:, None, :]
    sine = jnp.sin(angles)[:, None, :]
    first_half = values_in[..., :half_size]
    second_half = values_in[..., half_size:]
    return jnp.concatenate([first_half * cosine - second_half * sine, second_half * cosine + first_half * sine], axis=-1)

def reference(hidden_in, gain_in, w_query, query_scale, w_key, key_scale, w_value, value_scale, w_out, out_scale, gain_mid, head_order):
    hidden_f = hidden_in.astype(jnp.float32)
    inverse = lax.rsqrt(lax.optimization_barrier(jnp.mean(hidden_f * hidden_f, axis=1, keepdims=True)) + epsilon)
    normed = (hidden_f * inverse * gain_in[None, :]).astype(jnp.bfloat16)
    kept_heads = head_order[:KEEP].astype(jnp.int32)
    head_cols = (kept_heads[:, None] * HEAD + jnp.arange(HEAD, dtype=jnp.int32)[None, :]).reshape(-1)
    query_w = jnp.take(w_query, head_cols, axis=1)
    query = jnp.dot(normed, query_w, preferred_element_type=jnp.float32) * jnp.take(query_scale, head_cols)[None, :]
    keys = jnp.dot(normed, w_key, preferred_element_type=jnp.float32) * key_scale[None, :]
    values = (jnp.dot(normed, w_value, preferred_element_type=jnp.float32) * value_scale[None, :]).astype(jnp.bfloat16)
    positions = jnp.arange(TOKENS, dtype=jnp.int32) % L
    query = rotate(query.reshape(TOKENS, KEEP, HEAD), positions).astype(jnp.bfloat16)
    keys = rotate(keys.reshape(TOKENS, KVW, HEAD), positions).astype(jnp.bfloat16)
    values = values.reshape(TOKENS, KVW, HEAD)
    kv_index = (kept_heads // GROUP).astype(jnp.int32)
    keys = jnp.take(keys, kv_index, axis=1)
    values = jnp.take(values, kv_index, axis=1)
    causal = jnp.arange(L)[None, :] <= jnp.arange(L)[:, None]
    scale_factor = 1.0 / jnp.sqrt(jnp.float32(HEAD))

    def one_sequence(seq_index):
        first_row = (seq_index * L).astype(jnp.int32)
        query_seq = lax.dynamic_slice_in_dim(query, first_row, L, 0).astype(jnp.float32)
        key_seq = lax.dynamic_slice_in_dim(keys, first_row, L, 0).astype(jnp.float32)
        value_seq = lax.dynamic_slice_in_dim(values, first_row, L, 0).astype(jnp.float32)
        scores = jnp.einsum('qhd,khd->hqk', query_seq, key_seq) * scale_factor
        scores = jnp.where(causal[None], scores, -1e+30)
        weights = jax.nn.softmax(scores, axis=-1).astype(jnp.bfloat16)
        return jnp.einsum('hqk,khd->qhd', weights.astype(jnp.float32), value_seq).astype(jnp.bfloat16)
    attended = lax.map(one_sequence, jnp.arange(TOKENS // L, dtype=jnp.int32)).reshape(TOKENS, KEEP * HEAD)
    out_w = jnp.take(w_out, head_cols, axis=0)
    mixed = jnp.dot(attended, out_w, preferred_element_type=jnp.float32) * out_scale[None, :]
    residual_out = (hidden_f + mixed).astype(jnp.bfloat16)
    resid_f = residual_out.astype(jnp.float32)
    inverse_mid = lax.rsqrt(lax.optimization_barrier(jnp.mean(resid_f * resid_f, axis=1, keepdims=True)) + epsilon)
    ffn_input = (resid_f * inverse_mid * gain_mid[None, :]).astype(jnp.bfloat16)
    hessian = jnp.dot(ffn_input.T, ffn_input, preferred_element_type=jnp.float32) / TOKENS
    return (hessian, residual_out)
```

```python
import jax
import jax.numpy as jnp
import numpy as np
from jax import lax
from jax.experimental import pallas as pl
from jax.experimental.pallas import tpu as pltpu
from jax.sharding import Mesh
from jax.sharding import PartitionSpec as P

D = 16384
HEAD = 128
GROUP = 16
KVW = 2
L = 256
KEEP = 16
TOKENS = 2048
SEQ = 4
FSDP = 32
GT = TOKENS // SEQ
FW = D // FSDP
ROWS = GT // FSDP
QW = KEEP * HEAD
KV = KVW * HEAD
SW = QW + 2 * KV + 128

epsilon = 1e-05

AXES = ("yh", "core", "z", "x", "yl")
SIZES = (2, 2, 4, 4, 2)
TOK_AXES = ("yl", "z", "x")


bf16 = jnp.bfloat16
f32 = jnp.float32


def permute(array, move):
    places = np.array(list(np.ndindex(*SIZES)))
    pairs = [
        (int(np.ravel_multi_index(tuple(p), SIZES)), int(np.ravel_multi_index(move(*map(int, p)), SIZES)))
        for p in places
    ]
    return lax.ppermute(array, AXES, pairs)


def to_plane(yh, c, z, x, yl):
    return (z // 2, z % 2, 2 * yh + c, x, yl)


def along_first(d):
    def move(yh, c, z, x, yl):
        return (yh, c, (z + d) % 4, x, yl) if c == 0 else (yh, c, z, (x + d) % 4, yl)

    return move


def along_second(d):
    def move(yh, c, z, x, yl):
        return (yh, c, z, (x + d) % 4, yl) if c == 0 else (yh, c, (z + d) % 4, x, yl)

    return move


def other_yl(yh, c, z, x, yl):
    return (yh, c, z, x, 1 - yl)


def other_yh(yh, c, z, x, yl):
    return (1 - yh, c, z, x, yl)


def other_core(yh, c, z, x, yl):
    return (yh, 1 - c, z, x, yl)


def project_kernel(kept, h, g, wa, wb, wk, wv, sa, sb, ks, vs, out, hg):
    j = pl.program_id(0)

    @pl.when(j == 0)
    def _():
        hf = h[...].astype(f32)
        hg[...] = (hf * g[...]).astype(bf16)
        square = jnp.sum(hf * hf, axis=1, keepdims=True)
        high = square.astype(bf16).astype(f32)
        lane = lax.broadcasted_iota(jnp.int32, (GT, 128), 1)
        pad = jnp.where(lane == 0, high, jnp.where(lane == 1, square - high, 0.0))
        out[:, QW + 2 * KV :] = pad.astype(bf16)
        key = jnp.dot(hg[...], wk[...], preferred_element_type=f32) * ks[...]
        out[:, QW : QW + KV] = key.astype(bf16)
        value = jnp.dot(hg[...], wv[...], preferred_element_type=f32) * vs[...]
        out[:, QW + KV : QW + 2 * KV] = value.astype(bf16)

    w = jnp.concatenate([wa[...], wb[...]], axis=1)
    s = jnp.concatenate([sa[0], sb[0]], axis=1)
    q = jnp.dot(hg[...], w, preferred_element_type=f32) * s
    out[:, pl.ds(pl.multiple_of(j * 2 * HEAD, 2 * HEAD), 2 * HEAD)] = q.astype(bf16)


def project(kept, h, g, wq, qs, wk, ks, wv, vs):
    whole = lambda shape: pl.BlockSpec(shape, lambda j, kept: (0,) * len(shape))
    head = lambda i: pl.BlockSpec((FW, HEAD), lambda j, kept: (0, kept[2 * j + i]))
    scale = lambda i: pl.BlockSpec((1, 1, HEAD), lambda j, kept: (kept[2 * j + i], 0, 0))
    qs = qs.reshape(-1, 1, HEAD)
    return pl.pallas_call(
        project_kernel,
        out_shape=jax.ShapeDtypeStruct((GT, SW), bf16),
        grid_spec=pltpu.PrefetchScalarGridSpec(
            num_scalar_prefetch=1,
            grid=(KEEP // 2,),
            in_specs=[
                whole((GT, FW)),
                whole((1, FW)),
                head(0),
                head(1),
                whole((FW, KV)),
                whole((FW, KV)),
                scale(0),
                scale(1),
                whole((1, KV)),
                whole((1, KV)),
            ],
            out_specs=whole((GT, SW)),
            scratch_shapes=[pltpu.VMEM((GT, FW), bf16)],
        ),
    )(kept, h, g[None], wq, wq, wk, wv, qs, qs, ks[None], vs[None])


def rows_kernel(x, cosine, sine, q, kv):
    def column(j):
        return jnp.sum(x[:, :, j * 128 : (j + 1) * 128].astype(f32), axis=0)

    last = column((SW - 128) // 128)
    inverse = lax.rsqrt((last[:, 0:1] + last[:, 1:2]) / D + epsilon)
    cos, sin = cosine[...], sine[...]

    def rotated(j):
        v = column(j) * inverse
        return (v * cos + pltpu.roll(v, 64, axis=1) * sin).astype(bf16)

    for j in range(KEEP):
        q[:, j * 128 : (j + 1) * 128] = rotated(j)
    for j in range(2 * KVW):
        if j < KVW:
            part = rotated(KEEP + j)
        else:
            part = (column(KEEP + j) * inverse).astype(bf16)
        kv[:, :, j * 128 : (j + 1) * 128] = jnp.broadcast_to(part[None], (16, ROWS, 128))


def attend_kernel(q, kv, low, high, out):
    qs = jnp.concatenate([q[:, h * HEAD : (h + 1) * HEAD] for h in range(KEEP)], axis=0)
    keys = jnp.concatenate([kv[:, g * HEAD : (g + 1) * HEAD] for g in range(KVW)], axis=0)
    values = jnp.concatenate([kv[:, KV + g * HEAD : KV + (g + 1) * HEAD] for g in range(KVW)], axis=0)
    scores = lax.dot_general(qs, keys, (((1,), (1,)), ((), ())), preferred_element_type=f32)
    scores = scores * np.float32(1.0 / np.sqrt(HEAD))
    place = lax.broadcasted_iota(jnp.int32, scores.shape, 1)
    seen = (place >= low[...]) & (place <= high[...])
    scores = jnp.where(seen, scores, -1e30)
    top = jnp.max(scores, axis=1, keepdims=True)
    e = jnp.where(seen, jnp.exp(scores - top), 0.0)
    weights = (e / jnp.sum(e, axis=1, keepdims=True)).astype(bf16)
    att = jnp.dot(weights, values, preferred_element_type=f32).astype(bf16)
    for h in range(KEEP):
        part = att[h * ROWS : (h + 1) * ROWS]
        out[:, :, h * HEAD : (h + 1) * HEAD] = jnp.broadcast_to(part[None], (FSDP, ROWS, HEAD))


def mix_kernel(kept, att, wa, wb, scale, h, gain, residual, gained, acc):
    j = pl.program_id(0)
    a = att[:, pl.ds(pl.multiple_of(j * 2 * HEAD, 2 * HEAD), 2 * HEAD)]
    w = jnp.concatenate([wa[...], wb[...]], axis=0)
    part = jnp.dot(a, w, preferred_element_type=f32)

    @pl.when(j == 0)
    def _():
        acc[...] = part

    @pl.when(j > 0)
    def _():
        acc[...] += part

    @pl.when(j == KEEP // 2 - 1)
    def _():
        r = (h[...].astype(f32) + acc[...] * scale[...]).astype(bf16)
        residual[...] = r
        gained[...] = (r.astype(f32) * gain[...]).astype(bf16)


def mix(kept, att, w_out, out_scale, h, gain):
    whole = lambda shape: pl.BlockSpec(shape, lambda j, kept: (0,) * len(shape))
    head = lambda i: pl.BlockSpec((HEAD, FW), lambda j, kept: (kept[2 * j + i], 0))
    return pl.pallas_call(
        mix_kernel,
        out_shape=[jax.ShapeDtypeStruct((GT, FW), bf16)] * 2,
        grid_spec=pltpu.PrefetchScalarGridSpec(
            num_scalar_prefetch=1,
            grid=(KEEP // 2,),
            in_specs=[
                whole((GT, QW)),
                head(0),
                head(1),
                whole((1, FW)),
                whole((GT, FW)),
                whole((1, FW)),
            ],
            out_specs=[whole((GT, FW))] * 2,
            scratch_shapes=[pltpu.VMEM((GT, FW), f32)],
        ),
    )(kept, att, w_out, w_out, out_scale[None], h, gain[None])


def moment_kernel(count, first, *refs):
    table = refs[0]
    lhs = refs[1:5]
    chunks = refs[5 : 5 + count]
    refs = refs[5 + count :]
    if not first:
        before, refs = refs[0], refs[1:]
    out, acc, left, held, acc_sem, left_sem, held_sem = refs
    strip = lambda ref, i: ref.at[:, pl.ds(i * FW, FW)]
    reads = [pltpu.make_async_copy(lhs[i], left.at[i], left_sem.at[i]) for i in range(4)]
    reads += [pltpu.make_async_copy(chunks[i], held.at[i], held_sem.at[i]) for i in range(count)]
    if first:
        acc[...] = jnp.zeros_like(acc)
    else:
        reads = [pltpu.make_async_copy(strip(before, i), acc.at[i], acc_sem.at[i]) for i in range(8)] + reads
    for copy in reads:
        copy.start()
    for copy in reads[: len(reads) - count]:
        copy.wait()
    for i in range(count):
        reads[len(reads) - count + i].wait()
        group = table[i, 0]
        block = table[i, 1]
        acc[block] += jnp.dot(left[group], held[i], preferred_element_type=f32)
    writes = [pltpu.make_async_copy(acc.at[i], strip(out, i), acc_sem.at[i]) for i in range(8)]
    for copy in writes:
        copy.start()
    for copy in writes:
        copy.wait()


def moment(table, lhs, chunks, before=None):
    count = len(chunks)
    first = before is None
    anywhere = pl.BlockSpec(memory_space=pl.ANY)
    operands = [table, *lhs, *chunks] + ([] if first else [before])
    return pl.pallas_call(
        lambda *refs: moment_kernel(count, first, *refs),
        out_shape=jax.ShapeDtypeStruct((FW, D // SEQ), f32),
        in_specs=[pl.BlockSpec(memory_space=pltpu.SMEM)] + [anywhere] * (len(operands) - 1),
        out_specs=anywhere,
        scratch_shapes=[
            pltpu.VMEM((8, FW, FW), f32),
            pltpu.VMEM((4, FW, GT), bf16),
            pltpu.VMEM((count, GT, FW), bf16),
            pltpu.SemaphoreType.DMA((8,)),
            pltpu.SemaphoreType.DMA((4,)),
            pltpu.SemaphoreType.DMA((count,)),
        ],
        input_output_aliases={} if first else {len(operands) - 1: 0},
        name="moment_first" if first else "moment_rest",
    )(*operands)


def shards(
    hidden_in,
    gain_in,
    w_query,
    query_scale,
    w_key,
    key_scale,
    w_value,
    value_scale,
    w_out,
    out_scale,
    gain_mid,
    head_order,
):
    yh, core, z, x, yl = (lax.axis_index(a) for a in AXES)
    kept = head_order[:KEEP]

    partial = project(kept, hidden_in, gain_in, w_query, query_scale, w_key, key_scale, w_value, value_scale)
    received = lax.all_to_all(
        partial.reshape(FSDP, ROWS, SW), TOK_AXES, split_axis=0, concat_axis=0, tiled=True
    )

    positions = (z * 4 + x) * ROWS + jnp.arange(ROWS, dtype=jnp.int32)
    steps = jnp.arange(HEAD // 2, dtype=f32)
    frequency = jnp.exp(-jnp.log(jnp.float32(500000.0)) * steps * 2.0 / HEAD)
    angles = positions.astype(f32)[:, None] * frequency[None, :]
    cosine = jnp.cos(angles)
    sine = jnp.sin(angles)
    cosine = jnp.concatenate([cosine, cosine], axis=1)
    sine = jnp.concatenate([-sine, sine], axis=1)
    query, kv_own = pl.pallas_call(
        rows_kernel,
        out_shape=[
            jax.ShapeDtypeStruct((ROWS, QW), bf16),
            jax.ShapeDtypeStruct((16, ROWS, 2 * KV), bf16),
        ],
    )(received, cosine, sine)
    kv = lax.all_to_all(kv_own, ("z", "x"), split_axis=0, concat_axis=0, tiled=True)

    low = jnp.repeat(kept // GROUP * L, ROWS)[:, None]
    high = low + jnp.tile(positions, KEEP)[:, None]
    attended = pl.pallas_call(
        attend_kernel,
        out_shape=jax.ShapeDtypeStruct((FSDP, ROWS, QW), bf16),
    )(query, kv.reshape(L, 2 * KV), low, high)
    attended = lax.all_to_all(attended, TOK_AXES, split_axis=0, concat_axis=0, tiled=True)
    residual, gained = mix(kept, attended.reshape(GT, QW), w_out, out_scale, hidden_in, gain_mid)

    own = permute(gained, to_plane)
    pair = [own, permute(own, other_yl)]
    pieces = {}
    for e in range(2):
        a = [pair[e]] + [permute(pair[e], along_first(d)) for d in (1, -1, 2)]
        for i in range(4):
            pieces[i, e, 0] = a[i]
            pieces[i, e, 1] = permute(a[i], along_second(1))
            pieces[i, e, 2] = permute(a[i], along_second(-1))
            pieces[i, e, 3] = permute(pieces[i, e, 1 + e], along_second(1 - 2 * e))

    resid_f = residual.astype(f32)
    square = jnp.sum(resid_f * resid_f, axis=1)
    square = jnp.broadcast_to(square[None, None], (FSDP, 1, GT))
    square = lax.all_to_all(square, TOK_AXES, split_axis=0, concat_axis=0, tiled=True).sum(axis=(0, 1))
    weight = 1.0 / ((square / D + epsilon) * TOKENS)
    rows = (gained.T.astype(f32) * weight[None, :]).astype(bf16)
    rows_yh = permute(rows, other_yh)
    lhs = [rows, rows_yh, permute(rows, other_core), permute(rows_yh, other_core)]

    first_at = jnp.where(core == 0, z, x)
    second_at = jnp.where(core == 0, x, z)
    offsets = (0, -1, 1, 2)

    def entry(i, e, b):
        first = (first_at + offsets[i]) % 4
        second = (second_at + offsets[b]) % 4
        group = jnp.where(core == 0, first, second)
        x_at = jnp.where(core == 0, second, first)
        yl_at = yl if e == 0 else 1 - yl
        left = (group // 2 != yh).astype(jnp.int32) + 2 * (group % 2 != core).astype(jnp.int32)
        return [left, x_at * 2 + yl_at]

    def part(keys, before=None):
        table = jnp.stack([jnp.stack(entry(*k)) for k in keys]).astype(jnp.int32)
        return moment(table, lhs, [pieces[k] for k in keys], before)

    near = [k for k in pieces if k[2] < 3]
    far = [k for k in pieces if k[2] == 3]
    hessian = part(far, part(near))
    return (hessian, residual)


def solution(mesh):
    fine = Mesh(mesh.devices.reshape(SIZES), AXES)
    seq = ("yh", "core")
    fsdp = ("z", "x", "yl")
    return jax.shard_map(
        shards,
        mesh=fine,
        in_specs=(
            P(seq, fsdp),
            P(fsdp),
            P(fsdp, None),
            P(),
            P(fsdp, None),
            P(),
            P(fsdp, None),
            P(),
            P(None, fsdp),
            P(fsdp),
            P(fsdp),
            P(),
        ),
        out_specs=(P(fsdp, seq), P(seq, fsdp)),
        check_vma=False,
    )
```

```python
import jax
import jax.numpy as jnp
import numpy as np
from jax import lax
from jax.experimental import pallas as pl
from jax.experimental.pallas import tpu as pltpu
from jax.sharding import Mesh
from jax.sharding import PartitionSpec as P

D = 16384
HEAD = 128
GROUP = 16
KVW = 2
L = 256
KEEP = 16
TOKENS = 2048
SEQ = 4
FSDP = 32
GT = TOKENS // SEQ
FW = D // FSDP
ROWS = GT // FSDP
QW = KEEP * HEAD
KV = KVW * HEAD
STEP = 4
SW = QW + 2 * KV + 128

epsilon = 1e-05

AXES = ("yh", "core", "z", "x", "yl")
SIZES = (2, 2, 4, 4, 2)
TOK_AXES = ("yl", "z", "x")


bf16 = jnp.bfloat16
f32 = jnp.float32


def permute(array, move):
    places = np.array(list(np.ndindex(*SIZES)))
    pairs = [
        (int(np.ravel_multi_index(tuple(p), SIZES)), int(np.ravel_multi_index(move(*map(int, p)), SIZES)))
        for p in places
    ]
    return lax.ppermute(array, AXES, pairs)


def to_plane(yh, c, z, x, yl):
    return (z // 2, z % 2, 2 * yh + c, x, yl)


def along_first(d):
    def move(yh, c, z, x, yl):
        return (yh, c, (z + d) % 4, x, yl) if c == 0 else (yh, c, z, (x + d) % 4, yl)

    return move


def along_second(d):
    def move(yh, c, z, x, yl):
        return (yh, c, z, (x + d) % 4, yl) if c == 0 else (yh, c, (z + d) % 4, x, yl)

    return move


def other_yl(yh, c, z, x, yl):
    return (yh, c, z, x, 1 - yl)


def other_yh(yh, c, z, x, yl):
    return (1 - yh, c, z, x, yl)


def other_core(yh, c, z, x, yl):
    return (yh, 1 - c, z, x, yl)


def project_kernel(kept, h, g, *refs):
    ws, refs = refs[:STEP], refs[STEP:]
    wk, wv, *refs = refs
    ss, refs = refs[:STEP], refs[STEP:]
    ks, vs, out, hg = refs
    j = pl.program_id(0)

    @pl.when(j == 0)
    def _():
        hf = h[...].astype(f32)
        hg[...] = (hf * g[...]).astype(bf16)
        square = jnp.sum(hf * hf, axis=1, keepdims=True)
        high = square.astype(bf16).astype(f32)
        lane = lax.broadcasted_iota(jnp.int32, (GT, 128), 1)
        pad = jnp.where(lane == 0, high, jnp.where(lane == 1, square - high, 0.0))
        out[:, QW + 2 * KV :] = pad.astype(bf16)
        key = jnp.dot(hg[...], wk[...], preferred_element_type=f32) * ks[...]
        out[:, QW : QW + KV] = key.astype(bf16)
        value = jnp.dot(hg[...], wv[...], preferred_element_type=f32) * vs[...]
        out[:, QW + KV : QW + 2 * KV] = value.astype(bf16)

    w = jnp.concatenate([r[...] for r in ws], axis=1)
    s = jnp.concatenate([r[0] for r in ss], axis=1)
    q = jnp.dot(hg[...], w, preferred_element_type=f32) * s
    out[:, pl.ds(pl.multiple_of(j * STEP * HEAD, STEP * HEAD), STEP * HEAD)] = q.astype(bf16)


def project(kept, h, g, wq, qs, wk, ks, wv, vs):
    whole = lambda shape: pl.BlockSpec(shape, lambda j, kept: (0,) * len(shape))
    head = lambda i: pl.BlockSpec((FW, HEAD), lambda j, kept: (0, kept[STEP * j + i]))
    scale = lambda i: pl.BlockSpec((1, 1, HEAD), lambda j, kept: (kept[STEP * j + i], 0, 0))
    qs = qs.reshape(-1, 1, HEAD)
    return pl.pallas_call(
        project_kernel,
        out_shape=jax.ShapeDtypeStruct((GT, SW), bf16),
        grid_spec=pltpu.PrefetchScalarGridSpec(
            num_scalar_prefetch=1,
            grid=(KEEP // STEP,),
            in_specs=[
                whole((GT, FW)),
                whole((1, FW)),
                *[head(i) for i in range(STEP)],
                whole((FW, KV)),
                whole((FW, KV)),
                *[scale(i) for i in range(STEP)],
                whole((1, KV)),
                whole((1, KV)),
            ],
            out_specs=whole((GT, SW)),
            scratch_shapes=[pltpu.VMEM((GT, FW), bf16)],
        ),
    )(kept, h, g[None], *[wq] * STEP, wk, wv, *[qs] * STEP, ks[None], vs[None])


def rows_kernel(x, cosine, sine, q, kv):
    def column(j):
        return jnp.sum(x[:, :, j * 128 : (j + 1) * 128].astype(f32), axis=0)

    last = column((SW - 128) // 128)
    inverse = lax.rsqrt((last[:, 0:1] + last[:, 1:2]) / D + epsilon)
    cos, sin = cosine[...], sine[...]

    def rotated(j):
        v = column(j) * inverse
        return (v * cos + pltpu.roll(v, 64, axis=1) * sin).astype(bf16)

    for j in range(KEEP):
        q[:, j * 128 : (j + 1) * 128] = rotated(j)
    for j in range(2 * KVW):
        if j < KVW:
            part = rotated(KEEP + j)
        else:
            part = (column(KEEP + j) * inverse).astype(bf16)
        kv[:, :, j * 128 : (j + 1) * 128] = jnp.broadcast_to(part[None], (16, ROWS, 128))


def attend_kernel(q, kv, low, high, out):
    qs = jnp.concatenate([q[:, h * HEAD : (h + 1) * HEAD] for h in range(KEEP)], axis=0)
    keys = jnp.concatenate([kv[:, g * HEAD : (g + 1) * HEAD] for g in range(KVW)], axis=0)
    values = jnp.concatenate([kv[:, KV + g * HEAD : KV + (g + 1) * HEAD] for g in range(KVW)], axis=0)
    scores = lax.dot_general(qs, keys, (((1,), (1,)), ((), ())), preferred_element_type=f32)
    scores = scores * np.float32(1.0 / np.sqrt(HEAD))
    place = lax.broadcasted_iota(jnp.int32, scores.shape, 1)
    seen = (place >= low[...]) & (place <= high[...])
    scores = jnp.where(seen, scores, -1e30)
    top = jnp.max(scores, axis=1, keepdims=True)
    e = jnp.where(seen, jnp.exp(scores - top), 0.0)
    weights = (e / jnp.sum(e, axis=1, keepdims=True)).astype(bf16)
    att = jnp.dot(weights, values, preferred_element_type=f32).astype(bf16)
    for h in range(KEEP):
        part = att[h * ROWS : (h + 1) * ROWS]
        out[:, :, h * HEAD : (h + 1) * HEAD] = jnp.broadcast_to(part[None], (FSDP, ROWS, HEAD))


def mix_kernel(kept, att, *refs):
    ws, refs = refs[:STEP], refs[STEP:]
    scale, h, gain, residual, gained, acc = refs
    j = pl.program_id(0)
    a = att[:, pl.ds(pl.multiple_of(j * STEP * HEAD, STEP * HEAD), STEP * HEAD)]
    w = jnp.concatenate([r[...] for r in ws], axis=0)
    part = jnp.dot(a, w, preferred_element_type=f32)

    @pl.when(j == 0)
    def _():
        acc[...] = part

    @pl.when(j > 0)
    def _():
        acc[...] += part

    @pl.when(j == KEEP // STEP - 1)
    def _():
        r = (h[...].astype(f32) + acc[...] * scale[...]).astype(bf16)
        residual[...] = r
        gained[...] = (r.astype(f32) * gain[...]).astype(bf16)


def mix(kept, att, w_out, out_scale, h, gain):
    whole = lambda shape: pl.BlockSpec(shape, lambda j, kept: (0,) * len(shape))
    head = lambda i: pl.BlockSpec((HEAD, FW), lambda j, kept: (kept[STEP * j + i], 0))
    return pl.pallas_call(
        mix_kernel,
        out_shape=[jax.ShapeDtypeStruct((GT, FW), bf16)] * 2,
        grid_spec=pltpu.PrefetchScalarGridSpec(
            num_scalar_prefetch=1,
            grid=(KEEP // STEP,),
            in_specs=[
                whole((GT, QW)),
                *[head(i) for i in range(STEP)],
                whole((1, FW)),
                whole((GT, FW)),
                whole((1, FW)),
            ],
            out_specs=[whole((GT, FW))] * 2,
            scratch_shapes=[pltpu.VMEM((GT, FW), f32)],
        ),
    )(kept, att, *[w_out] * STEP, out_scale[None], h, gain[None])


def moment_kernel(sizes, slots, old, *refs):
    count = sum(sizes)
    table = refs[0]
    lhs = refs[1:5]
    groups = refs[5 : 5 + len(sizes)]
    refs = refs[5 + len(sizes) :]
    if old:
        before, refs = refs[0], refs[1:]
    out, acc, left, held, acc_sem, left_sem, held_sem, *past = refs

    def strip(ref, i):
        block = 2 * (i % 4) + table[count + i // 4, 0]
        return ref.at[:, pl.ds(pl.multiple_of(block * FW, FW), FW)]

    reads = [pltpu.make_async_copy(lhs[i], left.at[i], left_sem.at[i]) for i in range(4)]
    start = 0
    chunks = []
    for group, size in zip(groups, sizes):
        chunks.append(pltpu.make_async_copy(group, held.at[pl.ds(start, size)], held_sem.at[len(chunks)]))
        start += size
    for copy in reads + chunks:
        copy.start()
    if old:
        olds = [pltpu.make_async_copy(strip(before, i), past[0].at[i], acc_sem.at[i]) for i in range(slots)]
        for copy in olds:
            copy.start()
    acc[...] = jnp.zeros_like(acc)
    for copy in reads:
        copy.wait()
    start = 0
    for copy, size in zip(chunks, sizes):
        copy.wait()
        for i in range(start, start + size):
            acc[table[i, 1]] += jnp.dot(left[table[i, 0]], held[i], preferred_element_type=f32)
        start += size
    writes = [pltpu.make_async_copy(acc.at[i], strip(out, i), acc_sem.at[i]) for i in range(slots)]
    for i in range(slots):
        if old:
            olds[i].wait()
            acc[i] += past[0][i]
        writes[i].start()
    for copy in writes:
        copy.wait()


def moment(table, lhs, groups, before, slots):
    sizes = tuple(group.shape[0] for group in groups)
    count = sum(sizes)
    old = before is not None
    anywhere = pl.BlockSpec(memory_space=pl.ANY)
    operands = [table, *lhs, *groups] + ([before] if old else [])
    return pl.pallas_call(
        lambda *refs: moment_kernel(sizes, slots, old, *refs),
        out_shape=jax.ShapeDtypeStruct((FW, D // SEQ), f32),
        in_specs=[pl.BlockSpec(memory_space=pltpu.SMEM)] + [anywhere] * (len(operands) - 1),
        out_specs=anywhere,
        scratch_shapes=[
            pltpu.VMEM((slots, FW, FW), f32),
            pltpu.VMEM((4, FW, GT), bf16),
            pltpu.VMEM((count, GT, FW), bf16),
            pltpu.SemaphoreType.DMA((slots,)),
            pltpu.SemaphoreType.DMA((4,)),
            pltpu.SemaphoreType.DMA((len(sizes),)),
        ]
        + ([pltpu.VMEM((slots, FW, FW), f32)] if old else []),
        input_output_aliases={len(operands) - 1: 0} if old else {},
    )(*operands)


def shards(
    hidden_in,
    gain_in,
    w_query,
    query_scale,
    w_key,
    key_scale,
    w_value,
    value_scale,
    w_out,
    out_scale,
    gain_mid,
    head_order,
):
    yh, core, z, x, yl = (lax.axis_index(a) for a in AXES)
    kept = head_order[:KEEP]

    partial = project(kept, hidden_in, gain_in, w_query, query_scale, w_key, key_scale, w_value, value_scale)
    received = lax.all_to_all(
        partial.reshape(FSDP, ROWS, SW), TOK_AXES, split_axis=0, concat_axis=0, tiled=True
    )

    positions = (z * 4 + x) * ROWS + jnp.arange(ROWS, dtype=jnp.int32)
    steps = jnp.arange(HEAD // 2, dtype=f32)
    frequency = jnp.exp(-jnp.log(jnp.float32(500000.0)) * steps * 2.0 / HEAD)
    angles = positions.astype(f32)[:, None] * frequency[None, :]
    cosine = jnp.cos(angles)
    sine = jnp.sin(angles)
    cosine = jnp.concatenate([cosine, cosine], axis=1)
    sine = jnp.concatenate([-sine, sine], axis=1)
    query, kv_own = pl.pallas_call(
        rows_kernel,
        out_shape=[
            jax.ShapeDtypeStruct((ROWS, QW), bf16),
            jax.ShapeDtypeStruct((16, ROWS, 2 * KV), bf16),
        ],
    )(received, cosine, sine)
    kv = lax.all_to_all(kv_own, ("z", "x"), split_axis=0, concat_axis=0, tiled=True)

    low = jnp.repeat(kept // GROUP * L, ROWS)[:, None]
    high = low + jnp.tile(positions, KEEP)[:, None]
    attended = pl.pallas_call(
        attend_kernel,
        out_shape=jax.ShapeDtypeStruct((FSDP, ROWS, QW), bf16),
    )(query, kv.reshape(L, 2 * KV), low, high)
    attended = lax.all_to_all(attended, TOK_AXES, split_axis=0, concat_axis=0, tiled=True)
    residual, gained = mix(kept, attended.reshape(GT, QW), w_out, out_scale, hidden_in, gain_mid)

    resid_f = residual.astype(f32)
    square = jnp.sum(resid_f * resid_f, axis=1)
    square = jnp.broadcast_to(square[None, None], (FSDP, 1, GT))
    square = lax.all_to_all(square, TOK_AXES, split_axis=0, concat_axis=0, tiled=True)

    own = permute(gained, to_plane)
    pair = [own, permute(own, other_yl)]
    here, before, after, far = [], [], [], []
    for e in range(2):
        a = [pair[e]] + [permute(pair[e], along_first(d)) for d in (1, -1, 2)]
        here.append(jnp.stack(a))
        before.append(permute(here[e], along_second(1)))
        after.append(permute(here[e], along_second(-1)))
        far.append(permute(before[e][:2], along_second(1)))
        far.append(permute(after[e][2:], along_second(-1)))

    square = square.sum(axis=(0, 1))
    weight = 1.0 / ((square / D + epsilon) * TOKENS)
    rows = (gained.T.astype(f32) * weight[None, :]).astype(bf16)
    rows_yh = permute(rows, other_yh)
    lhs = [rows, rows_yh, permute(rows, other_core), permute(rows_yh, other_core)]

    first_at = jnp.where(core == 0, z, x)
    second_at = jnp.where(core == 0, x, z)
    offsets = np.array([0, -1, 1, 2], np.int32)

    def table_of(groups, shift):
        i = np.tile(np.arange(4), len(groups))
        e, b = (np.repeat(np.array(v), 4) for v in zip(*groups))
        first = (first_at + offsets[i]) % 4
        second = (second_at + offsets[b]) % 4
        group = jnp.where(core == 0, first, second)
        x_at = jnp.where(core == 0, second, first) + 4 * (e - shift)
        left = (group // 2 != yh).astype(jnp.int32) + 2 * (group % 2 != core).astype(jnp.int32)
        halves = jnp.stack([yl, 1 - yl][shift:] + [yl] * shift)
        body = jnp.stack([left, x_at], axis=1)
        return jnp.concatenate([body, jnp.stack([halves] * 2, axis=1)]).astype(jnp.int32)

    groups = [(0, 0), (1, 0), (0, 1), (0, 2)]
    hessian = moment(table_of(groups, 0), lhs, [here[0], here[1], before[0], after[0]], None, 8)
    groups = [(1, 1), (1, 2), (0, 3)]
    hessian = moment(table_of(groups, 0), lhs, [before[1], after[1], far[0], far[1]], hessian, 8)
    hessian = moment(table_of([(1, 3)], 1), lhs, [far[2], far[3]], hessian, 4)
    return (hessian, residual)


def solution(mesh):
    fine = Mesh(mesh.devices.reshape(SIZES), AXES)
    seq = ("yh", "core")
    fsdp = ("z", "x", "yl")
    return jax.shard_map(
        shards,
        mesh=fine,
        in_specs=(
            P(seq, fsdp),
            P(fsdp),
            P(fsdp, None),
            P(),
            P(fsdp, None),
            P(),
            P(fsdp, None),
            P(),
            P(None, fsdp),
            P(fsdp),
            P(fsdp),
            P(),
        ),
        out_specs=(P(fsdp, seq), P(seq, fsdp)),
        check_vma=False,
    )
```

```python
import jax
import jax.numpy as jnp
import numpy as np
from jax import lax
from jax.experimental import pallas as pl
from jax.experimental.pallas import tpu as pltpu
from jax.sharding import Mesh
from jax.sharding import PartitionSpec as P

D = 16384
HEAD = 128
GROUP = 16
KVW = 2
L = 256
KEEP = 16
TOKENS = 2048
SEQ = 4
FSDP = 32
GT = TOKENS // SEQ
FW = D // FSDP
ROWS = GT // FSDP
QW = KEEP * HEAD
KV = KVW * HEAD
STEP = 4

epsilon = 1e-05

AXES = ("yh", "core", "z", "x", "yl")
SIZES = (2, 2, 4, 4, 2)
TOK_AXES = ("yl", "z", "x")


bf16 = jnp.bfloat16
f32 = jnp.float32


def permute(array, move):
    places = np.array(list(np.ndindex(*SIZES)))
    pairs = [
        (int(np.ravel_multi_index(tuple(p), SIZES)), int(np.ravel_multi_index(move(*map(int, p)), SIZES)))
        for p in places
    ]
    return lax.ppermute(array, AXES, pairs)


def to_plane(yh, c, z, x, yl):
    return (z // 2, z % 2, (z + 2 * yh + c) % 4, x, yl)


def along_first(d):
    def move(yh, c, z, x, yl):
        return (yh, c, (z + d) % 4, x, yl) if c == 0 else (yh, c, z, (x + d) % 4, yl)

    return move


def along_second(d):
    def move(yh, c, z, x, yl):
        return (yh, c, z, (x + d) % 4, yl) if c == 0 else (yh, c, (z + d) % 4, x, yl)

    return move


def along_x(d):
    return lambda yh, c, z, x, yl: (yh, c, z, (x + d) % 4, yl)


def along_z(d):
    return lambda yh, c, z, x, yl: (yh, c, (z + d) % 4, x, yl)


def other_yl(yh, c, z, x, yl):
    return (yh, c, z, x, 1 - yl)


def other_yh(yh, c, z, x, yl):
    return (1 - yh, c, z, x, yl)


def other_core(yh, c, z, x, yl):
    return (yh, 1 - c, z, x, yl)


def narrow_kernel(h, g, wk, wv, ks, vs, out, hg):
    hf = h[...].astype(f32)
    hg[...] = (hf * g[...]).astype(bf16)
    square = jnp.sum(hf * hf, axis=1, keepdims=True)
    high = square.astype(bf16).astype(f32)
    lane = lax.broadcasted_iota(jnp.int32, (GT, 128), 1)
    pad = jnp.where(lane == 0, high, jnp.where(lane == 1, square - high, 0.0))
    out[:, 2 * KV :] = pad.astype(bf16)
    key = jnp.dot(hg[...], wk[...], preferred_element_type=f32) * ks[...]
    out[:, :KV] = key.astype(bf16)
    value = jnp.dot(hg[...], wv[...], preferred_element_type=f32) * vs[...]
    out[:, KV : 2 * KV] = value.astype(bf16)


def wide_kernel(kept, hg, *refs):
    ws, ss, (out,) = refs[:STEP], refs[STEP : 2 * STEP], refs[2 * STEP :]
    w = jnp.concatenate([r[...] for r in ws], axis=1)
    s = jnp.concatenate([r[0] for r in ss], axis=1)
    out[...] = (jnp.dot(hg[...], w, preferred_element_type=f32) * s).astype(bf16)


def wide(kept, hg, wq, qs):
    head = lambda i: pl.BlockSpec((FW, HEAD), lambda j, kept: (0, kept[STEP * j + i]))
    scale = lambda i: pl.BlockSpec((1, 1, HEAD), lambda j, kept: (kept[STEP * j + i], 0, 0))
    return pl.pallas_call(
        wide_kernel,
        out_shape=jax.ShapeDtypeStruct((GT, QW), bf16),
        grid_spec=pltpu.PrefetchScalarGridSpec(
            num_scalar_prefetch=1,
            grid=(KEEP // STEP,),
            in_specs=[pl.BlockSpec((GT, FW), lambda j, kept: (0, 0))]
            + [head(i) for i in range(STEP)]
            + [scale(i) for i in range(STEP)],
            out_specs=pl.BlockSpec((GT, STEP * HEAD), lambda j, kept: (0, j)),
        ),
    )(kept, hg, *[wq] * STEP, *[qs.reshape(-1, 1, HEAD)] * STEP)


def summed(x, j):
    return jnp.sum(x[:, :, j * 128 : (j + 1) * 128].astype(f32), axis=0)


def rotated(v, cosine, sine):
    return (v * cosine + pltpu.roll(v, 64, axis=1) * sine).astype(bf16)


def keys_kernel(x, cosine, sine, kv, inverse):
    last = summed(x, 2 * KVW)
    inv = lax.rsqrt((last[:, 0:1] + last[:, 1:2]) / D + epsilon)
    inverse[...] = jnp.broadcast_to(inv, (ROWS, 128))
    for j in range(2 * KVW):
        v = summed(x, j) * inv
        part = rotated(v, cosine[...], sine[...]) if j < KVW else v.astype(bf16)
        kv[:, j * 128 : (j + 1) * 128] = part


def attend_kernel(x, inverse, cosine, sine, kva, kvb, kvc, kvd, place, low, high, out):
    kv = jnp.concatenate([r[...].reshape(4 * ROWS, 2 * KV) for r in (kva, kvb, kvc, kvd)], axis=0)
    cos, sin = cosine[...] * inverse[...], sine[...] * inverse[...]
    qs = jnp.concatenate([rotated(summed(x, h), cos, sin) for h in range(KEEP)], axis=0)
    keys = jnp.concatenate([kv[:, g * HEAD : (g + 1) * HEAD] for g in range(KVW)], axis=0)
    values = jnp.concatenate([kv[:, KV + g * HEAD : KV + (g + 1) * HEAD] for g in range(KVW)], axis=0)
    scores = lax.dot_general(qs, keys, (((1,), (1,)), ((), ())), preferred_element_type=f32)
    scores = scores * np.float32(1.0 / np.sqrt(HEAD))
    seen = (place[...] >= low[...]) & (place[...] <= high[...])
    scores = jnp.where(seen, scores, -1e30)
    top = jnp.max(scores, axis=1, keepdims=True)
    e = jnp.where(seen, jnp.exp(scores - top), 0.0)
    weights = (e / jnp.sum(e, axis=1, keepdims=True)).astype(bf16)
    att = jnp.dot(weights, values, preferred_element_type=f32).astype(bf16)
    for h in range(KEEP):
        part = att[h * ROWS : (h + 1) * ROWS]
        out[:, :, h * HEAD : (h + 1) * HEAD] = jnp.broadcast_to(part[None], (FSDP, ROWS, HEAD))


def mix_kernel(kept, att, *refs):
    ws, refs = refs[:STEP], refs[STEP:]
    scale, h, gain, residual, gained, acc = refs
    j = pl.program_id(0)
    a = att[:, pl.ds(pl.multiple_of(j * STEP * HEAD, STEP * HEAD), STEP * HEAD)]
    w = jnp.concatenate([r[...] for r in ws], axis=0)
    part = jnp.dot(a, w, preferred_element_type=f32)

    @pl.when(j == 0)
    def _():
        acc[...] = part

    @pl.when(j > 0)
    def _():
        acc[...] += part

    @pl.when(j == KEEP // STEP - 1)
    def _():
        r = (h[...].astype(f32) + acc[...] * scale[...]).astype(bf16)
        residual[...] = r
        gained[...] = (r.astype(f32) * gain[...]).astype(bf16)


def mix(kept, att, w_out, out_scale, h, gain):
    whole = lambda shape: pl.BlockSpec(shape, lambda j, kept: (0,) * len(shape))
    head = lambda i: pl.BlockSpec((HEAD, FW), lambda j, kept: (kept[STEP * j + i], 0))
    return pl.pallas_call(
        mix_kernel,
        out_shape=[jax.ShapeDtypeStruct((GT, FW), bf16)] * 2,
        grid_spec=pltpu.PrefetchScalarGridSpec(
            num_scalar_prefetch=1,
            grid=(KEEP // STEP,),
            in_specs=[
                whole((GT, QW)),
                *[head(i) for i in range(STEP)],
                whole((1, FW)),
                whole((GT, FW)),
                whole((1, FW)),
            ],
            out_specs=[whole((GT, FW))] * 2,
            scratch_shapes=[pltpu.VMEM((GT, FW), f32)],
        ),
    )(kept, att, *[w_out] * STEP, out_scale[None], h, gain[None])


def moment_kernel(count, stage, *refs):
    table, refs = refs[0], refs[1:]
    lhs, refs = (refs[:4], refs[4:]) if stage == 0 else ((), refs)
    groups, refs = refs[:count], refs[count:]
    if stage == 0:
        left, out, held, held_sem, out_sem, acc = refs
    elif stage == 1:
        left, acc, held, held_sem, out_sem = refs
    else:
        left, _, _, acc, out, held, held_sem, out_sem = refs

    chunks = [pltpu.make_async_copy(groups[i], held.at[i], held_sem.at[i]) for i in range(count)]
    reads = [pltpu.make_async_copy(lhs[i], left.at[i], out_sem.at[i]) for i in range(len(lhs))]
    for copy in reads + chunks[:3]:
        copy.start()
    if stage < 2:
        acc[...] = jnp.zeros_like(acc)
    for copy in reads:
        copy.wait()
    for i in range(count):
        chunks[i].wait()
        if i + 3 < count:
            chunks[i + 3].start()
        for k in range(2):
            group, block = table[2 * i + k, 0], table[2 * i + k, 1]
            acc[block] += jnp.dot(left[group], held[i, k], preferred_element_type=f32)
    if stage == 1:
        return
    writes = []
    for n in range(4):
        block = 2 * n + table[2 * count, 0]
        strip = out.at[:, pl.ds(pl.multiple_of(block * FW, FW), FW)]
        writes.append(pltpu.make_async_copy(acc.at[n], strip, out_sem.at[n]))
        writes[-1].start()
    for copy in writes:
        copy.wait()


def moment(table, groups, state, stage):
    count = len(groups)
    anywhere = pl.BlockSpec(memory_space=pl.ANY)
    vmem = pl.BlockSpec(memory_space=pltpu.VMEM)
    left = pltpu.VMEM((4, FW, GT), bf16)
    sums = pltpu.VMEM((4, FW, FW), f32)
    hessian = jax.ShapeDtypeStruct((FW, D // SEQ), f32)
    scratch = [
        pltpu.VMEM((count, 2, GT, FW), bf16),
        pltpu.SemaphoreType.DMA((count,)),
        pltpu.SemaphoreType.DMA((4,)),
    ]
    if stage == 0:
        operands, specs = [*state, *groups], [anywhere] * (4 + count)
        out_shape, out_specs, aliases = [left, hessian], [vmem, anywhere], {}
        scratch.append(sums)
    elif stage == 1:
        operands, specs = [*groups, near(state[0])], [anywhere] * count + [vmem]
        out_shape, out_specs, aliases = [sums], [vmem], {}
    else:
        operands = [*groups, near(state[0]), near(state[1]), state[2]]
        specs = [anywhere] * count + [vmem, vmem, anywhere]
        out_shape, out_specs, aliases = [sums, hessian], [vmem, anywhere], {count + 2: 0, count + 3: 1}
    return pl.pallas_call(
        lambda *refs: moment_kernel(count, stage, *refs),
        out_shape=out_shape,
        in_specs=[pl.BlockSpec(memory_space=pltpu.SMEM)] + specs,
        out_specs=out_specs,
        scratch_shapes=scratch,
        input_output_aliases=aliases,
        compiler_params=pltpu.CompilerParams(vmem_limit_bytes=24 << 20),
    )(table, *operands)


def near(array):
    return pltpu.with_memory_space_constraint(array, pltpu.VMEM)


def shards(
    hidden_in,
    gain_in,
    w_query,
    query_scale,
    w_key,
    key_scale,
    w_value,
    value_scale,
    w_out,
    out_scale,
    gain_mid,
    head_order,
):
    yh, core, z, x, yl = (lax.axis_index(a) for a in AXES)
    kept = head_order[:KEEP]

    narrow, hg = pl.pallas_call(
        narrow_kernel,
        out_shape=[jax.ShapeDtypeStruct((GT, 2 * KV + 128), bf16), jax.ShapeDtypeStruct((GT, FW), bf16)],
    )(hidden_in, gain_in[None], w_key, w_value, key_scale[None], value_scale[None])
    narrow = lax.all_to_all(narrow.reshape(FSDP, ROWS, 2 * KV + 128), TOK_AXES, split_axis=0, concat_axis=0, tiled=True)
    query = wide(kept, hg, w_query, query_scale).reshape(FSDP, ROWS, QW)
    query = lax.all_to_all(query, TOK_AXES, split_axis=0, concat_axis=0, tiled=True)

    positions = (z * 4 + x) * ROWS + jnp.arange(ROWS, dtype=jnp.int32)
    steps = jnp.arange(HEAD // 2, dtype=f32)
    frequency = jnp.exp(-jnp.log(jnp.float32(500000.0)) * steps * 2.0 / HEAD)
    angles = positions.astype(f32)[:, None] * frequency[None, :]
    cosine = jnp.cos(angles)
    sine = jnp.sin(angles)
    cosine = jnp.concatenate([cosine, cosine], axis=1)
    sine = jnp.concatenate([-sine, sine], axis=1)
    kv_own, inverse = pl.pallas_call(
        keys_kernel,
        out_shape=[jax.ShapeDtypeStruct((ROWS, 2 * KV), bf16), jax.ShapeDtypeStruct((ROWS, 128), f32)],
    )(near(narrow), cosine, sine)
    kv = jnp.stack([kv_own] + [permute(kv_own, along_x(d)) for d in (1, -1, 2)])
    kv = [kv] + [permute(kv, along_z(d)) for d in (1, -1, 2)]

    offsets = np.array([0, -1, 1, 2], np.int32)
    block = ((z + offsets) % 4)[:, None] * 4 + ((x + offsets) % 4)[None, :]
    place = block.reshape(-1, 1) * ROWS + np.arange(ROWS, dtype=np.int32)[None, :]
    place = place.reshape(1, L) + np.arange(KVW, dtype=np.int32)[:, None] * L
    low = jnp.repeat(kept // GROUP * L, ROWS)[:, None]
    high = low + jnp.tile(positions, KEEP)[:, None]
    attended = pl.pallas_call(
        attend_kernel,
        out_shape=jax.ShapeDtypeStruct((FSDP, ROWS, QW), bf16),
    )(near(query), inverse, cosine, sine, *kv, place.reshape(1, KVW * L), low, high)
    attended = lax.all_to_all(attended, TOK_AXES, split_axis=0, concat_axis=0, tiled=True)
    residual, gained = mix(kept, attended.reshape(GT, QW), w_out, out_scale, hidden_in, gain_mid)

    resid_f = residual.astype(f32)
    square = jnp.sum(resid_f * resid_f, axis=1)
    square = jnp.broadcast_to(square[None, None], (FSDP, 1, GT))
    square = lax.all_to_all(square, TOK_AXES, split_axis=0, concat_axis=0, tiled=True)

    own = permute(gained, to_plane)
    other = permute(own, other_yl)
    a = [own] + [permute(own, along_first(d)) for d in (1, -1, 2)]
    pieces = {(0, 0, half): jnp.stack(a[2 * half : 2 * half + 2]) for half in range(2)}
    pieces[1, 0, 0] = jnp.stack([other, permute(a[1], other_yl)])
    pieces[1, 0, 1] = permute(pieces[0, 0, 1], other_yl)
    for e in range(2):
        for half in range(2):
            for b, d in ((1, 1), (2, -1)):
                pieces[e, b, half] = permute(pieces[e, 0, half], along_second(d))
        pieces[e, 3, 0] = permute(pieces[e, 1, 0], along_second(1))
        far = (pieces[0, 2, 1], along_second(-1)) if e == 0 else (pieces[0, 3, 1], other_yl)
        pieces[e, 3, 1] = permute(*far)

    square = square.sum(axis=(0, 1))
    weight = 1.0 / ((square / D + epsilon) * TOKENS)
    rows = (gained.T.astype(f32) * weight[None, :]).astype(bf16)
    rows_yh = permute(rows, other_yh)
    lhs = [rows, rows_yh, permute(rows, other_core), permute(rows_yh, other_core)]

    first_at = jnp.where(core == 0, z, x)
    second_at = jnp.where(core == 0, x, z)

    def table_of(keys):
        e, b, i = (np.array([k[j] if j < 2 else 2 * k[2] + n for k in keys for n in range(2)]) for j in range(3))
        first = (first_at + offsets[i]) % 4
        second = (second_at + offsets[b]) % 4
        group = (jnp.where(core == 0, first, second) - 2 * yh - core) % 4
        x_at = jnp.where(core == 0, second, first)
        left = (group // 2 != yh).astype(jnp.int32) + 2 * (group % 2 != core).astype(jnp.int32)
        half = yl if e[0] == 0 else 1 - yl
        return jnp.concatenate([jnp.stack([left, x_at], axis=1), jnp.full((1, 2), half)]).astype(jnp.int32)

    keys = [
        [(0, b, half) for b in range(4) for half in range(2)],
        [(1, 0, 0), (1, 0, 1), (1, 1, 0), (1, 2, 0), (1, 2, 1), (1, 3, 1)],
        [(1, 1, 1), (1, 3, 0)],
    ]
    tables = [table_of(k) for k in keys]
    groups = [[pieces[k] for k in ks] for ks in keys]
    left, hessian = moment(tables[0], groups[0], lhs, 0)
    (sums,) = moment(tables[1], groups[1], [left], 1)
    _, hessian = moment(tables[2], groups[2], [left, sums, hessian], 2)
    return (hessian, residual)


def solution(mesh):
    fine = Mesh(mesh.devices.reshape(SIZES), AXES)
    seq = ("yh", "core")
    fsdp = ("z", "x", "yl")
    return jax.shard_map(
        shards,
        mesh=fine,
        in_specs=(
            P(seq, fsdp),
            P(fsdp),
            P(fsdp, None),
            P(),
            P(fsdp, None),
            P(),
            P(fsdp, None),
            P(),
            P(None, fsdp),
            P(fsdp),
            P(fsdp),
            P(),
        ),
        out_specs=(P(fsdp, seq), P(seq, fsdp)),
        check_vma=False,
    )
```

```python
import jax
import jax.numpy as jnp
import numpy as np
from jax import lax
from jax.experimental import pallas as pl
from jax.experimental.pallas import tpu as pltpu
from jax.sharding import Mesh
from jax.sharding import PartitionSpec as P

D = 16384
HEAD = 128
GROUP = 16
KVW = 2
L = 256
KEEP = 16
TOKENS = 2048
SEQ = 4
FSDP = 32
GT = TOKENS // SEQ
FW = D // FSDP
ROWS = GT // FSDP
QW = KEEP * HEAD
KV = KVW * HEAD
STEP = 8

epsilon = 1e-05

AXES = ("yh", "core", "z", "x", "yl")
SIZES = (2, 2, 4, 4, 2)
TOK_AXES = ("yl", "z", "x")


bf16 = jnp.bfloat16
f32 = jnp.float32


def permute(array, move):
    places = np.array(list(np.ndindex(*SIZES)))
    pairs = [
        (int(np.ravel_multi_index(tuple(p), SIZES)), int(np.ravel_multi_index(move(*map(int, p)), SIZES)))
        for p in places
    ]
    return lax.ppermute(array, AXES, pairs)


def to_plane(yh, c, z, x, yl):
    return (z // 2, z % 2, (z + 2 * yh + c) % 4, x, yl)


def along_first(d):
    def move(yh, c, z, x, yl):
        return (yh, c, (z + d) % 4, x, yl) if c == 0 else (yh, c, z, (x + d) % 4, yl)

    return move


def along_second(d):
    def move(yh, c, z, x, yl):
        return (yh, c, z, (x + d) % 4, yl) if c == 0 else (yh, c, (z + d) % 4, x, yl)

    return move


def along_x(d):
    return lambda yh, c, z, x, yl: (yh, c, z, (x + d) % 4, yl)


def along_z(d):
    return lambda yh, c, z, x, yl: (yh, c, (z + d) % 4, x, yl)


def other_yl(yh, c, z, x, yl):
    return (yh, c, z, x, 1 - yl)


def other_yh(yh, c, z, x, yl):
    return (1 - yh, c, z, x, yl)


def other_core(yh, c, z, x, yl):
    return (yh, 1 - c, z, x, yl)


def narrow_kernel(h, g, wk, wv, ks, vs, out, hg):
    hf = h[...].astype(f32)
    hg[...] = (hf * g[...]).astype(bf16)
    square = jnp.sum(hf * hf, axis=1, keepdims=True)
    high = square.astype(bf16).astype(f32)
    lane = lax.broadcasted_iota(jnp.int32, (GT, 128), 1)
    pad = jnp.where(lane == 0, high, jnp.where(lane == 1, square - high, 0.0))
    out[:, 2 * KV :] = pad.astype(bf16)
    key = jnp.dot(hg[...], wk[...], preferred_element_type=f32) * ks[...]
    out[:, :KV] = key.astype(bf16)
    value = jnp.dot(hg[...], wv[...], preferred_element_type=f32) * vs[...]
    out[:, KV : 2 * KV] = value.astype(bf16)


def wide_kernel(kept, hg, *refs):
    ws, ss, (out,) = refs[:STEP], refs[STEP : 2 * STEP], refs[2 * STEP :]
    w = jnp.concatenate([r[...] for r in ws], axis=1)
    s = jnp.concatenate([r[0] for r in ss], axis=1)
    out[...] = (jnp.dot(hg[...], w, preferred_element_type=f32) * s).astype(bf16)


def wide(kept, hg, wq, qs):
    head = lambda i: pl.BlockSpec((FW, HEAD), lambda j, kept: (0, kept[STEP * j + i]))
    scale = lambda i: pl.BlockSpec((1, 1, HEAD), lambda j, kept: (kept[STEP * j + i], 0, 0))
    return pl.pallas_call(
        wide_kernel,
        out_shape=jax.ShapeDtypeStruct((GT, QW), bf16),
        grid_spec=pltpu.PrefetchScalarGridSpec(
            num_scalar_prefetch=1,
            grid=(KEEP // STEP,),
            in_specs=[pl.BlockSpec((GT, FW), lambda j, kept: (0, 0))]
            + [head(i) for i in range(STEP)]
            + [scale(i) for i in range(STEP)],
            out_specs=pl.BlockSpec((GT, STEP * HEAD), lambda j, kept: (0, j)),
        ),
    )(kept, hg, *[wq] * STEP, *[qs.reshape(-1, 1, HEAD)] * STEP)


def summed(x, j):
    return jnp.sum(x[:, :, j * 128 : (j + 1) * 128].astype(f32), axis=0)


def rotated(v, cosine, sine):
    return (v * cosine + pltpu.roll(v, 64, axis=1) * sine).astype(bf16)


def keys_kernel(x, cosine, sine, kv, inverse):
    last = summed(x, 2 * KVW)
    inv = lax.rsqrt((last[:, 0:1] + last[:, 1:2]) / D + epsilon)
    inverse[...] = jnp.broadcast_to(inv, (ROWS, 128))
    for j in range(2 * KVW):
        v = summed(x, j) * inv
        part = rotated(v, cosine[...], sine[...]) if j < KVW else v.astype(bf16)
        kv[:, j * 128 : (j + 1) * 128] = part


def attend_kernel(x, inverse, cosine, sine, kva, kvb, kvc, kvd, place, low, high, out):
    kv = jnp.concatenate([r[...].reshape(4 * ROWS, 2 * KV) for r in (kva, kvb, kvc, kvd)], axis=0)
    cos, sin = cosine[...] * inverse[...], sine[...] * inverse[...]
    qs = jnp.concatenate([rotated(summed(x, h), cos, sin) for h in range(KEEP)], axis=0)
    keys = jnp.concatenate([kv[:, g * HEAD : (g + 1) * HEAD] for g in range(KVW)], axis=0)
    values = jnp.concatenate([kv[:, KV + g * HEAD : KV + (g + 1) * HEAD] for g in range(KVW)], axis=0)
    scores = lax.dot_general(qs, keys, (((1,), (1,)), ((), ())), preferred_element_type=f32)
    scores = scores * np.float32(1.0 / np.sqrt(HEAD))
    seen = (place[...] >= low[...]) & (place[...] <= high[...])
    scores = jnp.where(seen, scores, -1e30)
    top = jnp.max(scores, axis=1, keepdims=True)
    e = jnp.where(seen, jnp.exp(scores - top), 0.0)
    weights = (e / jnp.sum(e, axis=1, keepdims=True)).astype(bf16)
    att = jnp.dot(weights, values, preferred_element_type=f32).astype(bf16)
    for h in range(KEEP):
        part = att[h * ROWS : (h + 1) * ROWS]
        out[:, :, h * HEAD : (h + 1) * HEAD] = jnp.broadcast_to(part[None], (FSDP, ROWS, HEAD))


def mix_kernel(kept, att, *refs):
    ws, refs = refs[:STEP], refs[STEP:]
    scale, h, gain, residual, gained, acc = refs
    j = pl.program_id(0)
    w = jnp.concatenate([r[...] for r in ws], axis=0)
    part = jnp.dot(att[...], w, preferred_element_type=f32)

    @pl.when(j == 0)
    def _():
        acc[...] = part

    @pl.when(j > 0)
    def _():
        acc[...] += part

    @pl.when(j == KEEP // STEP - 1)
    def _():
        r = (h[...].astype(f32) + acc[...] * scale[...]).astype(bf16)
        residual[...] = r
        gained[...] = (r.astype(f32) * gain[...]).astype(bf16)


def mix(kept, att, w_out, out_scale, h, gain):
    whole = lambda shape: pl.BlockSpec(shape, lambda j, kept: (0,) * len(shape))
    head = lambda i: pl.BlockSpec((HEAD, FW), lambda j, kept: (kept[STEP * j + i], 0))
    return pl.pallas_call(
        mix_kernel,
        out_shape=[jax.ShapeDtypeStruct((GT, FW), bf16)] * 2,
        grid_spec=pltpu.PrefetchScalarGridSpec(
            num_scalar_prefetch=1,
            grid=(KEEP // STEP,),
            in_specs=[
                pl.BlockSpec((GT, STEP * HEAD), lambda j, kept: (0, j)),
                *[head(i) for i in range(STEP)],
                whole((1, FW)),
                whole((GT, FW)),
                whole((1, FW)),
            ],
            out_specs=[whole((GT, FW))] * 2,
            scratch_shapes=[pltpu.VMEM((GT, FW), f32)],
        ),
    )(kept, att, *[w_out] * STEP, out_scale[None], h, gain[None])


def moment_kernel(count, stage, *refs):
    table, refs = refs[0], refs[1:]
    lhs, refs = (refs[:4], refs[4:]) if stage == 0 else ((), refs)
    groups, refs = refs[:count], refs[count:]
    if stage == 0:
        left, out, held, held_sem, out_sem, acc = refs
    elif stage == 1:
        left, acc, held, held_sem, out_sem = refs
    else:
        left, _, _, acc, out, held, held_sem, out_sem = refs

    chunks = [pltpu.make_async_copy(groups[i], held.at[i], held_sem.at[i]) for i in range(count)]
    reads = [pltpu.make_async_copy(lhs[i], left.at[i], out_sem.at[i]) for i in range(len(lhs))]
    for copy in reads + chunks[:3]:
        copy.start()
    if stage < 2:
        acc[...] = jnp.zeros_like(acc)
    for copy in reads:
        copy.wait()
    for i in range(count):
        chunks[i].wait()
        if i + 3 < count:
            chunks[i + 3].start()
        for k in range(2):
            group, block = table[2 * i + k, 0], table[2 * i + k, 1]
            acc[block] += jnp.dot(left[group], held[i, k], preferred_element_type=f32)
    if stage == 1:
        return
    writes = []
    for n in range(4):
        block = 2 * n + table[2 * count, 0]
        strip = out.at[:, pl.ds(pl.multiple_of(block * FW, FW), FW)]
        writes.append(pltpu.make_async_copy(acc.at[n], strip, out_sem.at[n]))
        writes[-1].start()
    for copy in writes:
        copy.wait()


def moment(table, groups, state, stage):
    count = len(groups)
    anywhere = pl.BlockSpec(memory_space=pl.ANY)
    vmem = pl.BlockSpec(memory_space=pltpu.VMEM)
    left = pltpu.VMEM((4, FW, GT), bf16)
    sums = pltpu.VMEM((4, FW, FW), f32)
    hessian = jax.ShapeDtypeStruct((FW, D // SEQ), f32)
    scratch = [
        pltpu.VMEM((count, 2, GT, FW), bf16),
        pltpu.SemaphoreType.DMA((count,)),
        pltpu.SemaphoreType.DMA((4,)),
    ]
    if stage == 0:
        operands, specs = [*state, *groups], [anywhere] * (4 + count)
        out_shape, out_specs, aliases = [left, hessian], [vmem, anywhere], {}
        scratch.append(sums)
    elif stage == 1:
        operands, specs = [*groups, near(state[0])], [anywhere] * count + [vmem]
        out_shape, out_specs, aliases = [sums], [vmem], {}
    else:
        operands = [*groups, near(state[0]), near(state[1]), state[2]]
        specs = [anywhere] * count + [vmem, vmem, anywhere]
        out_shape, out_specs, aliases = [sums, hessian], [vmem, anywhere], {count + 2: 0, count + 3: 1}
    return pl.pallas_call(
        lambda *refs: moment_kernel(count, stage, *refs),
        out_shape=out_shape,
        in_specs=[pl.BlockSpec(memory_space=pltpu.SMEM)] + specs,
        out_specs=out_specs,
        scratch_shapes=scratch,
        input_output_aliases=aliases,
        compiler_params=pltpu.CompilerParams(vmem_limit_bytes=24 << 20),
    )(table, *operands)


def near(array):
    return pltpu.with_memory_space_constraint(array, pltpu.VMEM)


def shards(
    hidden_in,
    gain_in,
    w_query,
    query_scale,
    w_key,
    key_scale,
    w_value,
    value_scale,
    w_out,
    out_scale,
    gain_mid,
    head_order,
):
    yh, core, z, x, yl = (lax.axis_index(a) for a in AXES)
    kept = head_order[:KEEP]

    narrow, hg = pl.pallas_call(
        narrow_kernel,
        out_shape=[jax.ShapeDtypeStruct((GT, 2 * KV + 128), bf16), jax.ShapeDtypeStruct((GT, FW), bf16)],
    )(hidden_in, gain_in[None], w_key, w_value, key_scale[None], value_scale[None])
    narrow = lax.all_to_all(narrow.reshape(FSDP, ROWS, 2 * KV + 128), TOK_AXES, split_axis=0, concat_axis=0, tiled=True)
    query = wide(kept, hg, w_query, query_scale).reshape(FSDP, ROWS, QW)
    query = lax.all_to_all(query, TOK_AXES, split_axis=0, concat_axis=0, tiled=True)

    positions = (z * 4 + x) * ROWS + jnp.arange(ROWS, dtype=jnp.int32)
    steps = jnp.arange(HEAD // 2, dtype=f32)
    frequency = jnp.exp(-jnp.log(jnp.float32(500000.0)) * steps * 2.0 / HEAD)
    angles = positions.astype(f32)[:, None] * frequency[None, :]
    cosine = jnp.cos(angles)
    sine = jnp.sin(angles)
    cosine = jnp.concatenate([cosine, cosine], axis=1)
    sine = jnp.concatenate([-sine, sine], axis=1)
    kv_own, inverse = pl.pallas_call(
        keys_kernel,
        out_shape=[jax.ShapeDtypeStruct((ROWS, 2 * KV), bf16), jax.ShapeDtypeStruct((ROWS, 128), f32)],
    )(near(narrow), cosine, sine)
    kv = jnp.stack([kv_own] + [permute(kv_own, along_x(d)) for d in (1, -1, 2)])
    kv = [kv] + [permute(kv, along_z(d)) for d in (1, -1, 2)]

    offsets = np.array([0, -1, 1, 2], np.int32)
    block = ((z + offsets) % 4)[:, None] * 4 + ((x + offsets) % 4)[None, :]
    place = block.reshape(-1, 1) * ROWS + np.arange(ROWS, dtype=np.int32)[None, :]
    place = place.reshape(1, L) + np.arange(KVW, dtype=np.int32)[:, None] * L
    low = jnp.repeat(kept // GROUP * L, ROWS)[:, None]
    high = low + jnp.tile(positions, KEEP)[:, None]
    attended = pl.pallas_call(
        attend_kernel,
        out_shape=jax.ShapeDtypeStruct((FSDP, ROWS, QW), bf16),
    )(near(query), inverse, cosine, sine, *kv, place.reshape(1, KVW * L), low, high)
    attended = lax.all_to_all(attended, TOK_AXES, split_axis=0, concat_axis=0, tiled=True)
    residual, gained = mix(kept, attended.reshape(GT, QW), w_out, out_scale, hidden_in, gain_mid)

    resid_f = residual.astype(f32)
    square = jnp.sum(resid_f * resid_f, axis=1)
    square = jnp.broadcast_to(square[None, None], (FSDP, 1, GT))
    square = lax.all_to_all(square, TOK_AXES, split_axis=0, concat_axis=0, tiled=True)

    own = permute(gained, to_plane)
    other = permute(own, other_yl)
    a = [own] + [permute(own, along_first(d)) for d in (1, -1, 2)]
    pieces = {(0, 0, half): jnp.stack(a[2 * half : 2 * half + 2]) for half in range(2)}
    crossed = permute(a[1], other_yl)
    pieces[1, 0, 0] = jnp.stack([other, crossed])
    pieces[1, 0, 1] = permute(pieces[0, 0, 1], other_yl)
    for e in range(2):
        for half in range(2):
            for b, d in ((1, 1), (2, -1)):
                pieces[e, b, half] = permute(pieces[e, 0, half], along_second(d))
        pieces[e, 3, 0] = permute(pieces[e, 1, 0], along_second(1))
        far = (pieces[0, 2, 1], along_second(-1)) if e == 0 else (pieces[0, 3, 1], other_yl)
        pieces[e, 3, 1] = permute(*far)

    square = square.sum(axis=(0, 1))
    weight = 1.0 / ((square / D + epsilon) * TOKENS)
    rows = (gained.T.astype(f32) * weight[None, :]).astype(bf16)
    rows_yh = permute(rows, other_yh)
    lhs = [rows, rows_yh, permute(rows, other_core), permute(rows_yh, other_core)]

    first_at = jnp.where(core == 0, z, x)
    second_at = jnp.where(core == 0, x, z)

    def table_of(keys):
        e, b, i = (np.array([k[j] if j < 2 else 2 * k[2] + n for k in keys for n in range(2)]) for j in range(3))
        first = (first_at + offsets[i]) % 4
        second = (second_at + offsets[b]) % 4
        group = (jnp.where(core == 0, first, second) - 2 * yh - core) % 4
        x_at = jnp.where(core == 0, second, first)
        left = (group // 2 != yh).astype(jnp.int32) + 2 * (group % 2 != core).astype(jnp.int32)
        half = yl if e[0] == 0 else 1 - yl
        return jnp.concatenate([jnp.stack([left, x_at], axis=1), jnp.full((1, 2), half)]).astype(jnp.int32)

    keys = [
        [(0, b, half) for b in range(4) for half in range(2)],
        [(1, 0, 0), (1, 0, 1), (1, 1, 0), (1, 2, 0), (1, 2, 1), (1, 3, 1)],
        [(1, 1, 1), (1, 3, 0)],
    ]
    tables = [table_of(k) for k in keys]
    groups = [[pieces[k] for k in ks] for ks in keys]
    left, hessian = moment(tables[0], groups[0], lhs, 0)
    (sums,) = moment(tables[1], groups[1], [left], 1)
    _, hessian = moment(tables[2], groups[2], [left, sums, hessian], 2)
    return (hessian, residual)


def solution(mesh):
    fine = Mesh(mesh.devices.reshape(SIZES), AXES)
    seq = ("yh", "core")
    fsdp = ("z", "x", "yl")
    return jax.shard_map(
        shards,
        mesh=fine,
        in_specs=(
            P(seq, fsdp),
            P(fsdp),
            P(fsdp, None),
            P(),
            P(fsdp, None),
            P(),
            P(fsdp, None),
            P(),
            P(None, fsdp),
            P(fsdp),
            P(fsdp),
            P(),
        ),
        out_specs=(P(fsdp, seq), P(seq, fsdp)),
        check_vma=False,
    )
```
